512 devices in a mesh: dp: 32 (over y_hi, z), inblk: 4 (over x), outcol: 4 (over y_lo, core).
Axes of the slice: x: 4, y: 8 (y_hi: 4, y_lo: 2; y = y_hi * 2 + y_lo), z: 8, core: 2. Of those that a mesh axis runs over, the one named last changes fastest.
Arguments:
- activations: bfloat16 [4096, 8192], P('dp', ('inblk', 'outcol')), may hold values from -1.5 to 1.5
- cotangent: bfloat16 [4096, 1024], P('dp', 'outcol'), may hold values from -6 to 6
- base_weight: bfloat16 [8192, 1024], P('inblk', 'outcol'), may hold values from -0.09375 to 0.09375
- skew_param: float32 [32, 256, 256], P(('inblk', 'outcol'), 'dp'), may hold values from -0.3125 to 0.3125
Outputs:
- grad_acts: bfloat16 [4096, 8192], P('dp', ('inblk', 'outcol'))
- grad_skew: float32 [32, 256, 256], P(('inblk', 'outcol'), 'dp')
The draws below stay inside these ranges and needn't reach their ends.
All inputs are finite; a program needn't handle non-finite values.
Results may differ from the reference program's by a relative error of at most 0.0058.
Values may be sent and summed in bfloat16 or wider, within the bound.
No kernel may reach another device: no remote copies, remote signals or barrier semaphores. Data moves between devices by JAX's collectives and lax.ppermute only.
A program may use at most 64 MiB of HBM per device.

```python
import jax
import jax.numpy as jnp
from jax import lax

D = 8192
KV = 1024
BLOCK = 256
TOKENS = 4096
BLOCKS = 32


def strengthened(array, stream_key, source, target, parts, factor):
    owner, partner = [(jnp.arange(array.shape[axis_at]) // (array.shape[axis_at] // parts)).reshape([-1 if axis == axis_at else 1 for axis in range(array.ndim)]) for axis_at in (source, target)]
    chosen = jax.random.permutation(stream_key, parts)[partner]
    strong = (owner == chosen) | (owner == (partner + parts // 2) % parts)
    return jnp.where(strong, factor * array, array)


def level_of(own_key, shape, shards, smallest, high):
    def one(dim, parts):
        draws = jax.random.uniform(jax.random.fold_in(jax.random.fold_in(own_key, 6), dim), (parts,), jnp.float32, smallest / len(shards), high / len(shards))
        return jnp.repeat(jnp.exp(draws), shape[dim] // parts).reshape((-1,) + (1,) * (len(shape) - dim - 1))

    level = one(*shards[0])
    for cut in shards[1:]:
        level = level * one(*cut)
    return level


def bell_draw(stream_key, dims, scale, bound, cuts=(), kind=jnp.bfloat16):
    drawn = jax.random.normal(stream_key, dims, jnp.float32) * scale
    if len(cuts) > 0:
        drawn = level_of(stream_key, dims, cuts, -0.22, 0.18) * drawn
    return jnp.clip(drawn, min=-bound, max=bound).astype(kind)


def gaussian_with(own_key, shape, width, most, pieces, heavy, kind=jnp.bfloat16):
    result = width * jax.random.normal(own_key, shape, jnp.float32)
    if pieces:
        result = result * level_of(own_key, shape, pieces, -0.22, 0.18)
    return jnp.clip(strengthened(result, jax.random.fold_in(own_key, 3), *heavy), -most, most).astype(kind)


def setup_inputs(seed: int = 0) -> dict:
    key_of = jax.random.split(jax.random.key(seed), 5)
    activations = bell_draw(key_of[0], (TOKENS, D), 0.1, 1.5, ((0, 32), (1, 16)))
    cotangent = bell_draw(key_of[1], (TOKENS, KV), 1.0, 6.0, ((0, 32), (1, 4)))
    base_weight = gaussian_with(key_of[2], (D, KV), D ** -0.5, 0.09375, ((0, 4), (1, 4)), (1, 0, 4, 2.0))
    skew_param = bell_draw(key_of[3], (BLOCKS, BLOCK, BLOCK), 0.02, 0.3125, ((0, 16), (1, 32)), jnp.float32)
    return dict(activations=activations, cotangent=cotangent, base_weight=base_weight, skew_param=skew_param)


def high_product(left, right):
    return jnp.matmul(left, right, precision=lax.Precision.HIGHEST)


def power_list(skew_input):
    skew_mat = skew_input - jnp.swapaxes(skew_input, -1, -2)
    powers = [skew_mat]
    for degree in range(5):
        powers.append(high_product(powers[-1], skew_mat))
    return powers


def rotation_of(powers):
    block_width = powers[0].shape[-1]
    identity_mat = jnp.eye(block_width, dtype=jnp.float32)
    series = powers[0] + powers[1] + powers[2] + powers[3] + powers[4]
    return identity_mat + 2.0 * series + powers[5]


def chain_rule(grad_rot, powers):
    negated = [powers[degree] * ((-1.0) ** (degree + 1)) for degree in range(5)]
    partial_value = grad_rot
    running = 2.0 * grad_rot
    for degree in range(2, 7):
        partial_value = high_product(negated[0], partial_value) + high_product(grad_rot, negated[degree - 2])
        weight_factor = 2.0 if degree < 6 else 1.0
        running = running + weight_factor * partial_value
    return running - jnp.swapaxes(running, -1, -2)


def reference(activations, cotangent, base_weight, skew_param):
    features = jnp.dot(cotangent, base_weight.T, preferred_element_type=jnp.float32).astype(jnp.bfloat16)

    def per_block(block_idx):
        offset = (block_idx * BLOCK).astype(jnp.int32)
        inputs = lax.dynamic_slice_in_dim(activations, offset, BLOCK, 1)
        block_feat = lax.dynamic_slice_in_dim(features, offset, BLOCK, 1)
        skew_block = lax.dynamic_index_in_dim(skew_param, block_idx, 0, keepdims=False)
        powers = power_list(skew_block)
        rotation = rotation_of(powers).astype(jnp.bfloat16)
        grad_block = jnp.dot(block_feat, rotation.T, preferred_element_type=jnp.float32).astype(jnp.bfloat16)
        grad_rot = jnp.dot(inputs.T, block_feat, preferred_element_type=jnp.float32)
        return grad_block, chain_rule(grad_rot, powers)

    grad_blocks, grad_skew = lax.map(per_block, jnp.arange(D // BLOCK, dtype=jnp.int32))
    grad_acts = jnp.transpose(grad_blocks, (1, 0, 2)).reshape(TOKENS, D)
    return grad_acts, grad_skew
```

```python
import jax
import jax.numpy as jnp
from jax import lax
from jax.experimental import pallas as pl
from jax.experimental.pallas import tpu as pltpu
from jax.sharding import PartitionSpec as P

BF16 = jnp.bfloat16
F32 = jnp.float32


def split(x):
    high = x.astype(BF16)
    return high, (x - high.astype(F32)).astype(BF16)


def product(left, right):
    dot = lambda a, b: jnp.dot(a, b, preferred_element_type=F32)
    return dot(left[0], right[0]) + (dot(left[0], right[1]) + dot(left[1], right[0]))


def factors(gathered, block):
    width = gathered.shape[-1]
    param = gathered[:, block].reshape(width, width)
    skew = param - param.T
    skew_pair = split(skew)
    square = product(skew_pair, skew_pair)
    square_pair = split(square)
    fourth = product(square_pair, square_pair)
    return skew, skew_pair, square, square_pair, square + fourth


def features_kernel(cotangent_ref, weight_ref, out_ref):
    out_ref[0] = lax.dot_general(
        cotangent_ref[...], weight_ref[...], (((1,), (1,)), ((), ())), preferred_element_type=F32
    ).astype(BF16)


def block_grad_kernel(parts_ref, acts_ref, features_ref, grad_ref):
    blocks, width = grad_ref.shape[0], grad_ref.shape[-1]
    total = parts_ref[0].astype(F32)
    for part in range(1, parts_ref.shape[0]):
        total = total + parts_ref[part].astype(F32)
    features = total.astype(BF16)
    features_ref[...] = features
    acts = acts_ref[...]
    for block in range(blocks):
        cols = slice(block * width, (block + 1) * width)
        grad_ref[block] = lax.dot_general(
            acts[:, cols], features[:, cols], (((0,), (0,)), ((), ())), preferred_element_type=F32
        )


def chain_kernel(gathered_ref, grad_ref, out_ref):
    shares, blocks, rows, width = gathered_ref.shape
    pieces = []
    for block in range(blocks):
        skew, skew_pair, square, square_pair, rest = factors(gathered_ref, block)
        grad = grad_ref[block]
        grad_pair = split(grad)
        left_bar = grad + product(grad_pair, split(rest))
        right_bar = grad + product(split(square - 2.0 * skew), grad_pair)
        right_sym = right_bar + right_bar.T
        both = left_bar + product(split(right_sym), square_pair)
        square_sym = right_sym + both + both.T
        total = 2.0 * left_bar - product(split(square_sym), skew_pair)
        pieces.append((total - total.T).reshape(shares, rows, width))
    out_ref[...] = jnp.concatenate(pieces, axis=1).astype(BF16)


def acts_kernel(gathered_ref, features_ref, out_ref):
    blocks, width = gathered_ref.shape[1], gathered_ref.shape[-1]
    for block in range(blocks):
        skew, _, square, _, rest = factors(gathered_ref, block)
        first = 2.0 * skew + square
        row = lax.broadcasted_iota(jnp.int32, (width, width), 0)
        col = lax.broadcasted_iota(jnp.int32, (width, width), 1)
        identity = jnp.where(row == col, 1.0, 0.0).astype(F32)
        rotation = (identity + first + rest + product(split(first), split(rest))).astype(BF16)
        cols = slice(block * width, (block + 1) * width)
        out_ref[:, cols] = lax.dot_general(
            features_ref[:, cols], rotation, (((1,), (1,)), ((), ())), preferred_element_type=F32
        ).astype(BF16)


def sum_kernel(parts_ref, out_ref):
    out_ref[...] = jnp.sum(parts_ref[...].astype(F32), axis=0)


def body(activations, cotangent, base_weight, skew_param):
    shares = lax.axis_size("dp")
    parts = lax.axis_size("outcol")
    tokens, own_width = activations.shape
    depth = cotangent.shape[1]
    blocks, rows, width = skew_param.shape
    gathered = lax.all_to_all(
        jnp.broadcast_to(skew_param[None], (shares, blocks, rows, width)), "dp", 0, 0, tiled=True
    )
    partial = pl.pallas_call(
        features_kernel,
        grid=(parts,),
        in_specs=[
            pl.BlockSpec((tokens, depth), lambda i: (0, 0)),
            pl.BlockSpec((own_width, depth), lambda i: (i, 0)),
        ],
        out_specs=pl.BlockSpec((1, tokens, own_width), lambda i: (i, 0, 0)),
        out_shape=jax.ShapeDtypeStruct((parts, tokens, own_width), BF16),
        cost_estimate=pl.CostEstimate(
            flops=2 * tokens * depth * own_width * parts, bytes_accessed=1 << 21, transcendentals=0
        ),
    )(cotangent, base_weight)
    received = lax.all_to_all(partial, "outcol", 0, 0, tiled=True)
    features, grad_rot = pl.pallas_call(
        block_grad_kernel,
        out_shape=(
            jax.ShapeDtypeStruct((tokens, own_width), BF16),
            jax.ShapeDtypeStruct((blocks, width, width), F32),
        ),
        cost_estimate=pl.CostEstimate(
            flops=2 * tokens * own_width * width, bytes_accessed=1 << 21, transcendentals=0
        ),
    )(received, activations)
    sends = pl.pallas_call(
        chain_kernel,
        out_shape=jax.ShapeDtypeStruct((shares, blocks * rows, width), BF16),
        cost_estimate=pl.CostEstimate(
            flops=2 * 18 * blocks * width**3, bytes_accessed=3 << 20, transcendentals=0
        ),
    )(gathered, grad_rot)
    arrived = lax.all_to_all(sends, "dp", 0, 0, tiled=True)
    grad_acts = pl.pallas_call(
        acts_kernel,
        out_shape=jax.ShapeDtypeStruct((tokens, own_width), BF16),
        cost_estimate=pl.CostEstimate(
            flops=2 * 10 * blocks * width**3, bytes_accessed=1 << 20, transcendentals=0
        ),
    )(gathered, features)
    grad_skew = pl.pallas_call(
        sum_kernel,
        out_shape=jax.ShapeDtypeStruct((blocks * rows, width), F32),
    )(arrived).reshape(blocks, rows, width)
    return grad_acts, grad_skew


def solution(mesh):
    return jax.shard_map(
        body,
        mesh=mesh,
        in_specs=(
            P("dp", ("inblk", "outcol")),
            P("dp", "outcol"),
            P("inblk", "outcol"),
            P(("inblk", "outcol"), "dp", None),
        ),
        out_specs=(P("dp", ("inblk", "outcol")), P(("inblk", "outcol"), "dp", None)),
        check_vma=False,
    )
```

```python
import jax
import jax.numpy as jnp
from jax import lax
from jax.experimental import pallas as pl
from jax.experimental.pallas import tpu as pltpu
from jax.sharding import PartitionSpec as P

BF16 = jnp.bfloat16
F32 = jnp.float32


def split(x):
    high = x.astype(BF16)
    return high, (x - high.astype(F32)).astype(BF16)


def product(left, right):
    dot = lambda a, b: jnp.dot(a, b, preferred_element_type=F32)
    return dot(left[0], right[0]) + (dot(left[0], right[1]) + dot(left[1], right[0]))


def factors(gathered, block):
    width = gathered.shape[-1]
    param = gathered[:, block].reshape(width, width)
    skew = param - param.T
    skew_pair = split(skew)
    square = product(skew_pair, skew_pair)
    square_pair = split(square)
    fourth = product(square_pair, square_pair)
    return skew, skew_pair, square, square_pair, square + fourth


def features_kernel(cotangent_ref, weight_ref, own_ref, *sent_refs):
    width = own_ref.shape[1]
    me = lax.axis_index("outcol")
    for turn in range(1 + len(sent_refs)):
        first = pl.multiple_of((me ^ turn) * width, width)
        part = lax.dot_general(
            cotangent_ref[...],
            weight_ref[pl.ds(first, width), :],
            (((1,), (1,)), ((), ())),
            preferred_element_type=F32,
        )
        if turn:
            sent_refs[turn - 1][...] = part.astype(BF16)
        else:
            own_ref[...] = part


def block_grad_kernel(acts_ref, own_ref, *refs):
    part_refs, (features_ref, grad_ref) = refs[:-2], refs[-2:]
    blocks, width = grad_ref.shape[0], grad_ref.shape[-1]
    total = own_ref[...]
    for part_ref in part_refs:
        total = total + part_ref[...].astype(F32)
    features = total.astype(BF16)
    features_ref[...] = features
    acts = acts_ref[...]
    for block in range(blocks):
        cols = slice(block * width, (block + 1) * width)
        grad_ref[block] = lax.dot_general(
            acts[:, cols], features[:, cols], (((0,), (0,)), ((), ())), preferred_element_type=F32
        )


def chain_kernel(gathered_ref, grad_ref, out_ref):
    shares, blocks, rows, width = gathered_ref.shape
    pieces = []
    for block in range(blocks):
        skew, skew_pair, square, square_pair, rest = factors(gathered_ref, block)
        grad = grad_ref[block]
        grad_pair = split(grad)
        left_bar = grad + product(grad_pair, split(rest))
        right_bar = grad + product(split(square - 2.0 * skew), grad_pair)
        right_sym = right_bar + right_bar.T
        both = left_bar + product(split(right_sym), square_pair)
        square_sym = right_sym + both + both.T
        total = 2.0 * left_bar - product(split(square_sym), skew_pair)
        pieces.append((total - total.T).reshape(shares, rows, width))
    out_ref[...] = jnp.concatenate(pieces, axis=1).astype(BF16)


def acts_kernel(gathered_ref, features_ref, out_ref):
    blocks, width = gathered_ref.shape[1], gathered_ref.shape[-1]
    for block in range(blocks):
        skew, _, square, _, rest = factors(gathered_ref, block)
        first = 2.0 * skew + square
        row = lax.broadcasted_iota(jnp.int32, (width, width), 0)
        col = lax.broadcasted_iota(jnp.int32, (width, width), 1)
        identity = jnp.where(row == col, 1.0, 0.0).astype(F32)
        rotation = (identity + first + rest + product(split(first), split(rest))).astype(BF16)
        cols = slice(block * width, (block + 1) * width)
        out_ref[:, cols] = lax.dot_general(
            features_ref[:, cols], rotation, (((1,), (1,)), ((), ())), preferred_element_type=F32
        ).astype(BF16)


def kernel_call(kernel, out_shape, flops, moved):
    return pl.pallas_call(
        kernel,
        out_shape=out_shape,
        compiler_params=pltpu.CompilerParams(vmem_limit_bytes=24 << 20),
        cost_estimate=pl.CostEstimate(flops=flops, bytes_accessed=moved, transcendentals=0),
    )


def body(activations, cotangent, base_weight, skew_param):
    shares = lax.axis_size("dp")
    parts = lax.axis_size("outcol")
    tokens, own_width = activations.shape
    depth = cotangent.shape[1]
    blocks, rows, width = skew_param.shape
    scale = 65536.0
    packed = (skew_param * scale).astype(jnp.float16)
    gathered = lax.all_to_all(
        jnp.broadcast_to(packed.reshape(1, blocks * rows, width), (shares, blocks * rows, width)),
        "dp",
        0,
        0,
        tiled=True,
    )
    gathered = (gathered.astype(F32) * (1.0 / scale)).reshape(shares, blocks, rows, width)
    own, *sent = kernel_call(
        features_kernel,
        [jax.ShapeDtypeStruct((tokens, own_width), F32)]
        + [jax.ShapeDtypeStruct((tokens, own_width), BF16)] * (parts - 1),
        2 * tokens * depth * own_width * parts,
        2 << 20,
    )(cotangent, base_weight)
    received = [
        lax.ppermute(part, "outcol", [(i, i ^ turn) for i in range(parts)])
        for turn, part in enumerate(sent, 1)
    ]
    features, grad_rot = kernel_call(
        block_grad_kernel,
        (
            jax.ShapeDtypeStruct((tokens, own_width), BF16),
            jax.ShapeDtypeStruct((blocks, width, width), F32),
        ),
        2 * tokens * own_width * width,
        2 << 20,
    )(activations, own, *received)
    sends = kernel_call(
        chain_kernel,
        jax.ShapeDtypeStruct((shares, blocks * rows, width), BF16),
        2 * 18 * blocks * width**3,
        2 << 20,
    )(gathered, grad_rot)
    arrived = lax.all_to_all(sends, "dp", 0, 0, tiled=True)
    grad_acts = kernel_call(
        acts_kernel,
        jax.ShapeDtypeStruct((tokens, own_width), BF16),
        2 * 10 * blocks * width**3,
        1 << 20,
    )(gathered, features)
    grad_skew = jnp.sum(arrived.astype(F32), axis=0).reshape(blocks, rows, width)
    return grad_acts, grad_skew


def solution(mesh):
    return jax.shard_map(
        body,
        mesh=mesh,
        in_specs=(
            P("dp", ("inblk", "outcol")),
            P("dp", "outcol"),
            P("inblk", "outcol"),
            P(("inblk", "outcol"), "dp", None),
        ),
        out_specs=(P("dp", ("inblk", "outcol")), P(("inblk", "outcol"), "dp", None)),
        check_vma=False,
    )
```

```python
import jax
import jax.numpy as jnp
from jax import lax
from jax.experimental import pallas as pl
from jax.experimental.pallas import tpu as pltpu
from jax.sharding import PartitionSpec as P

BF16 = jnp.bfloat16
F32 = jnp.float32


def split(x):
    high = x.astype(BF16)
    return high, (x - high.astype(F32)).astype(BF16)


def product(left, right):
    dot = lambda a, b: jnp.dot(a, b, preferred_element_type=F32)
    return dot(left[0], right[0]) + (dot(left[0], right[1]) + dot(left[1], right[0]))


def factors(gathered, block):
    width = gathered.shape[-1]
    param = gathered[:, block].reshape(width, width)
    skew = param - param.T
    skew_pair = split(skew)
    square = product(skew_pair, skew_pair)
    square_pair = split(square)
    fourth = product(square_pair, square_pair)
    return skew, skew_pair, square, square_pair, square + fourth


def features_kernel(cotangent_ref, weight_ref, own_ref, *refs):
    sent_refs, held, semaphores = refs[:-2], refs[-2], refs[-1]
    width = own_ref.shape[1]
    me = lax.axis_index("outcol")
    turns = range(len(sent_refs), -1, -1)
    copies = {}
    for turn in turns:
        first = pl.multiple_of((me ^ turn) * width, width)
        copies[turn] = pltpu.make_async_copy(
            weight_ref.at[pl.ds(first, width), :], held.at[turn], semaphores.at[turn]
        )
        copies[turn].start()
    for turn in turns:
        copies[turn].wait()
        part = lax.dot_general(
            cotangent_ref[...],
            held[turn],
            (((1,), (1,)), ((), ())),
            preferred_element_type=F32,
        )
        if turn:
            sent_refs[turn - 1][...] = part.astype(BF16)
        else:
            own_ref[...] = part


def block_grad_kernel(acts_ref, own_ref, *refs):
    part_refs, (features_ref, grad_ref) = refs[:-2], refs[-2:]
    blocks, width = grad_ref.shape[0], grad_ref.shape[-1]
    total = own_ref[...]
    for part_ref in part_refs:
        total = total + part_ref[...].astype(F32)
    features = total.astype(BF16)
    features_ref[...] = features
    acts = acts_ref[...]
    for block in range(blocks):
        cols = slice(block * width, (block + 1) * width)
        grad_ref[block] = lax.dot_general(
            acts[:, cols], features[:, cols], (((0,), (0,)), ((), ())), preferred_element_type=F32
        )


def chain_kernel(gathered_ref, grad_ref, out_ref):
    shares, blocks, rows, width = gathered_ref.shape
    every = range(blocks)
    param = [gathered_ref[:, b].reshape(width, width) for b in every]
    skew = [param[b] - param[b].T for b in every]
    skew_pair = [split(skew[b]) for b in every]
    square = [product(skew_pair[b], skew_pair[b]) for b in every]
    square_pair = [split(square[b]) for b in every]
    grad = [grad_ref[b] for b in every]
    grad_pair = [split(grad[b]) for b in every]
    right_bar = [
        grad[b] + product(split(square[b] - 2.0 * skew[b]), grad_pair[b]) for b in every
    ]
    fourth = [product(square_pair[b], square_pair[b]) for b in every]
    left_bar = [grad[b] + product(grad_pair[b], split(square[b] + fourth[b])) for b in every]
    right_sym = [right_bar[b] + right_bar[b].T for b in every]
    both = [left_bar[b] + product(split(right_sym[b]), square_pair[b]) for b in every]
    square_sym = [right_sym[b] + both[b] + both[b].T for b in every]
    total = [2.0 * left_bar[b] - product(split(square_sym[b]), skew_pair[b]) for b in every]
    pieces = [(total[b] - total[b].T).reshape(shares, rows, width) for b in every]
    out_ref[...] = jnp.concatenate(pieces, axis=1).astype(BF16)


def acts_kernel(gathered_ref, features_ref, out_ref):
    blocks, width = gathered_ref.shape[1], gathered_ref.shape[-1]
    for block in range(blocks):
        skew, _, square, _, rest = factors(gathered_ref, block)
        first = 2.0 * skew + square
        row = lax.broadcasted_iota(jnp.int32, (width, width), 0)
        col = lax.broadcasted_iota(jnp.int32, (width, width), 1)
        identity = jnp.where(row == col, 1.0, 0.0).astype(F32)
        rotation = (identity + first + rest + product(split(first), split(rest))).astype(BF16)
        cols = slice(block * width, (block + 1) * width)
        out_ref[:, cols] = lax.dot_general(
            features_ref[:, cols], rotation, (((1,), (1,)), ((), ())), preferred_element_type=F32
        ).astype(BF16)


def kernel_call(kernel, out_shape, flops, moved, **specs):
    return pl.pallas_call(
        kernel,
        out_shape=out_shape,
        compiler_params=pltpu.CompilerParams(vmem_limit_bytes=24 << 20),
        cost_estimate=pl.CostEstimate(flops=flops, bytes_accessed=moved, transcendentals=0),
        **specs,
    )


def body(activations, cotangent, base_weight, skew_param):
    shares = lax.axis_size("dp")
    parts = lax.axis_size("outcol")
    tokens, own_width = activations.shape
    depth = cotangent.shape[1]
    blocks, rows, width = skew_param.shape
    scale = 65536.0
    packed = (skew_param * scale).astype(jnp.float16).reshape(1, blocks * rows, width)
    gathered = lax.all_to_all(
        jnp.broadcast_to(packed, (shares, blocks * rows, width)), "dp", 0, 0, tiled=True
    )
    gathered = (gathered.astype(F32) * (1.0 / scale)).reshape(shares, blocks, rows, width)
    own, *sent = kernel_call(
        features_kernel,
        [jax.ShapeDtypeStruct((tokens, own_width), F32)]
        + [jax.ShapeDtypeStruct((tokens, own_width), BF16)] * (parts - 1),
        2 * tokens * depth * own_width * parts,
        2 << 20,
        in_specs=[pl.BlockSpec(memory_space=pltpu.VMEM), pl.BlockSpec(memory_space=pltpu.HBM)],
        scratch_shapes=[
            pltpu.VMEM((parts, own_width, depth), BF16),
            pltpu.SemaphoreType.DMA((parts,)),
        ],
    )(cotangent, pltpu.with_memory_space_constraint(base_weight, pltpu.HBM))
    received = [
        lax.ppermute(sent[turn - 1], "outcol", [(i, i ^ turn) for i in range(parts)])
        for turn in range(parts - 1, 0, -1)
    ]
    features, grad_rot = kernel_call(
        block_grad_kernel,
        (
            jax.ShapeDtypeStruct((tokens, own_width), BF16),
            jax.ShapeDtypeStruct((blocks, width, width), F32),
        ),
        2 * tokens * own_width * width,
        2 << 20,
    )(activations, own, *received)
    sends = kernel_call(
        chain_kernel,
        jax.ShapeDtypeStruct((shares, blocks * rows, width), BF16),
        2 * 18 * blocks * width**3,
        2 << 20,
    )(gathered, grad_rot)
    arrived = lax.all_to_all(sends, "dp", 0, 0, tiled=True)
    grad_acts = kernel_call(
        acts_kernel,
        jax.ShapeDtypeStruct((tokens, own_width), BF16),
        2 * 10 * blocks * width**3,
        1 << 20,
    )(gathered, features)
    grad_skew = jnp.sum(arrived.astype(F32), axis=0).reshape(blocks, rows, width)
    return grad_acts, grad_skew


def solution(mesh):
    return jax.shard_map(
        body,
        mesh=mesh,
        in_specs=(
            P("dp", ("inblk", "outcol")),
            P("dp", "outcol"),
            P("inblk", "outcol"),
            P(("inblk", "outcol"), "dp", None),
        ),
        out_specs=(P("dp", ("inblk", "outcol")), P(("inblk", "outcol"), "dp", None)),
        check_vma=False,
    )
```

```python
import jax
import jax.numpy as jnp
from jax import lax
from jax.experimental import pallas as pl
from jax.experimental.pallas import tpu as pltpu
from jax.sharding import PartitionSpec as P

BF16 = jnp.bfloat16
F32 = jnp.float32


def split(x):
    high = x.astype(BF16)
    return high, (x - high.astype(F32)).astype(BF16)


def product(left, right):
    dot = lambda a, b: jnp.dot(a, b, preferred_element_type=F32)
    return dot(left[0], right[0]) + (dot(left[0], right[1]) + dot(left[1], right[0]))


def factors(gathered, block):
    width = gathered.shape[-1]
    param = gathered[:, block].reshape(width, width)
    skew = param - param.T
    skew_pair = split(skew)
    square = product(skew_pair, skew_pair)
    square_pair = split(square)
    fourth = product(square_pair, square_pair)
    return skew, skew_pair, square, square_pair, square + fourth


def partial_sum(cotangent, weight):
    return lax.dot_general(
        cotangent, weight, (((1,), (1,)), ((), ())), preferred_element_type=F32
    )


def sent_kernel(cotangent_ref, weight_ref, out_ref, held, semaphores):
    width = out_ref.shape[-1]
    partner = lax.axis_index("outcol") ^ 1
    copies = []
    for half in range(out_ref.shape[0]):
        first = pl.multiple_of((partner ^ (2 * half)) * width, width)
        copies.append(
            pltpu.make_async_copy(
                weight_ref.at[pl.ds(first, width), :], held.at[half], semaphores.at[half]
            )
        )
        copies[half].start()
    for half in range(out_ref.shape[0]):
        copies[half].wait()
        out_ref[half] = partial_sum(cotangent_ref[...], held[half]).astype(BF16)


def kept_kernel(cotangent_ref, weight_ref, other_ref, own_ref, sent_ref):
    width = own_ref.shape[-1]
    me = lax.axis_index("outcol")
    for half, out_ref in ((1, sent_ref), (0, own_ref)):
        first = pl.multiple_of((me ^ (2 * half)) * width, width)
        part = partial_sum(cotangent_ref[...], weight_ref[pl.ds(first, width), :])
        out_ref[...] = (part + other_ref[half].astype(F32)).astype(out_ref.dtype)


def block_grad_kernel(acts_ref, own_ref, other_ref, features_ref, grad_ref):
    blocks, width = grad_ref.shape[0], grad_ref.shape[-1]
    features = (own_ref[...] + other_ref[...].astype(F32)).astype(BF16)
    features_ref[...] = features
    acts = acts_ref[...]
    for block in range(blocks):
        cols = slice(block * width, (block + 1) * width)
        grad_ref[block] = lax.dot_general(
            acts[:, cols], features[:, cols], (((0,), (0,)), ((), ())), preferred_element_type=F32
        )


def chain_kernel(gathered_ref, grad_ref, out_ref):
    shares, blocks, rows, width = gathered_ref.shape
    every = range(blocks)
    param = [gathered_ref[:, b].reshape(width, width) for b in every]
    skew = [param[b] - param[b].T for b in every]
    skew_pair = [split(skew[b]) for b in every]
    square = [product(skew_pair[b], skew_pair[b]) for b in every]
    square_pair = [split(square[b]) for b in every]
    grad = [grad_ref[b] for b in every]
    grad_pair = [split(grad[b]) for b in every]
    right_bar = [
        grad[b] + product(split(square[b] - 2.0 * skew[b]), grad_pair[b]) for b in every
    ]
    fourth = [product(square_pair[b], square_pair[b]) for b in every]
    left_bar = [grad[b] + product(grad_pair[b], split(square[b] + fourth[b])) for b in every]
    right_sym = [right_bar[b] + right_bar[b].T for b in every]
    both = [left_bar[b] + product(split(right_sym[b]), square_pair[b]) for b in every]
    square_sym = [right_sym[b] + both[b] + both[b].T for b in every]
    total = [2.0 * left_bar[b] - product(split(square_sym[b]), skew_pair[b]) for b in every]
    pieces = [(total[b] - total[b].T).reshape(shares, rows, width) for b in every]
    out_ref[...] = jnp.concatenate(pieces, axis=1).astype(BF16)


def acts_kernel(gathered_ref, features_ref, out_ref):
    blocks, width = gathered_ref.shape[1], gathered_ref.shape[-1]
    for block in range(blocks):
        skew, _, square, _, rest = factors(gathered_ref, block)
        first = 2.0 * skew + square
        row = lax.broadcasted_iota(jnp.int32, (width, width), 0)
        col = lax.broadcasted_iota(jnp.int32, (width, width), 1)
        identity = jnp.where(row == col, 1.0, 0.0).astype(F32)
        rotation = (identity + first + rest + product(split(first), split(rest))).astype(BF16)
        cols = slice(block * width, (block + 1) * width)
        out_ref[:, cols] = lax.dot_general(
            features_ref[:, cols], rotation, (((1,), (1,)), ((), ())), preferred_element_type=F32
        ).astype(BF16)


def kernel_call(kernel, out_shape, flops, moved, **specs):
    return pl.pallas_call(
        kernel,
        out_shape=out_shape,
        compiler_params=pltpu.CompilerParams(vmem_limit_bytes=24 << 20),
        cost_estimate=pl.CostEstimate(flops=flops, bytes_accessed=moved, transcendentals=0),
        **specs,
    )


def body(activations, cotangent, base_weight, skew_param):
    shares = lax.axis_size("dp")
    parts = lax.axis_size("outcol")
    tokens, own_width = activations.shape
    depth = cotangent.shape[1]
    blocks, rows, width = skew_param.shape
    scale = 65536.0
    shape = (shares, blocks * rows, width)
    place = lax.broadcasted_iota(jnp.int32, shape, 0) + lax.broadcasted_iota(jnp.int32, shape, 2)
    copies = jnp.where(place < 0, 0.0, skew_param.reshape(1, blocks * rows, width)) * scale
    gathered = lax.all_to_all(copies.astype(jnp.float16), "dp", 0, 0, tiled=True)
    gathered = (gathered.astype(F32) * (1.0 / scale)).reshape(shares, blocks, rows, width)
    vmem = pl.BlockSpec(memory_space=pltpu.VMEM)
    flops = tokens * depth * own_width * parts
    to_core = kernel_call(
        sent_kernel,
        jax.ShapeDtypeStruct((parts // 2, tokens, own_width), BF16),
        flops,
        1 << 20,
        in_specs=[vmem, pl.BlockSpec(memory_space=pltpu.HBM)],
        scratch_shapes=[
            pltpu.VMEM((parts // 2, own_width, depth), BF16),
            pltpu.SemaphoreType.DMA((parts // 2,)),
        ],
    )(cotangent, pltpu.with_memory_space_constraint(base_weight, pltpu.HBM))
    from_core = lax.ppermute(to_core, "outcol", [(i, i ^ 1) for i in range(parts)])
    own, to_chip = kernel_call(
        kept_kernel,
        (
            jax.ShapeDtypeStruct((tokens, own_width), F32),
            jax.ShapeDtypeStruct((tokens, own_width), BF16),
        ),
        flops,
        1 << 20,
    )(cotangent, base_weight, from_core)
    received = [lax.ppermute(to_chip, "outcol", [(i, i ^ 2) for i in range(parts)])]
    features, grad_rot = kernel_call(
        block_grad_kernel,
        (
            jax.ShapeDtypeStruct((tokens, own_width), BF16),
            jax.ShapeDtypeStruct((blocks, width, width), F32),
        ),
        2 * tokens * own_width * width,
        2 << 20,
    )(activations, own, *received)
    sends = kernel_call(
        chain_kernel,
        jax.ShapeDtypeStruct((shares, blocks * rows, width), BF16),
        2 * 18 * blocks * width**3,
        2 << 20,
    )(gathered, grad_rot)
    arrived = lax.all_to_all(sends, "dp", 0, 0, tiled=True)
    grad_acts = kernel_call(
        acts_kernel,
        jax.ShapeDtypeStruct((tokens, own_width), BF16),
        2 * 10 * blocks * width**3,
        1 << 20,
    )(gathered, features)
    grad_skew = jnp.sum(arrived.astype(F32), axis=0).reshape(blocks, rows, width)
    return grad_acts, grad_skew


def solution(mesh):
    return jax.shard_map(
        body,
        mesh=mesh,
        in_specs=(
            P("dp", ("inblk", "outcol")),
            P("dp", "outcol"),
            P("inblk", "outcol"),
            P(("inblk", "outcol"), "dp", None),
        ),
        out_specs=(P("dp", ("inblk", "outcol")), P(("inblk", "outcol"), "dp", None)),
        check_vma=False,
    )
```

```python
import jax
import jax.numpy as jnp
from jax import lax
from jax.experimental import pallas as pl
from jax.experimental.pallas import tpu as pltpu
from jax.sharding import PartitionSpec as P

BF16 = jnp.bfloat16
F32 = jnp.float32


def split(x):
    high = x.astype(BF16)
    return high, (x - high.astype(F32)).astype(BF16)


def product(left, right):
    dot = lambda a, b: jnp.dot(a, b, preferred_element_type=F32)
    return dot(left[0], right[0]) + (dot(left[0], right[1]) + dot(left[1], right[0]))


def factors(gathered, block):
    width = gathered.shape[-1]
    param = gathered[:, block].reshape(width, width)
    skew = param - param.T
    skew_pair = split(skew)
    square = product(skew_pair, skew_pair)
    square_pair = split(square)
    fourth = product(square_pair, square_pair)
    return skew, skew_pair, square, square_pair, square + fourth


def features_kernel(cotangent_ref, weight_ref, own_ref, *refs):
    sent_refs, held, semaphores = refs[:-2], refs[-2], refs[-1]
    width = own_ref.shape[1]
    me = lax.axis_index("outcol")
    turns = range(len(sent_refs), -1, -1)
    copies = {}
    for turn in turns:
        first = pl.multiple_of((me ^ turn) * width, width)
        copies[turn] = pltpu.make_async_copy(
            weight_ref.at[pl.ds(first, width), :], held.at[turn], semaphores.at[turn]
        )
        copies[turn].start()
    for turn in turns:
        copies[turn].wait()
        part = lax.dot_general(
            cotangent_ref[...],
            held[turn],
            (((1,), (1,)), ((), ())),
            preferred_element_type=F32,
        )
        if turn:
            sent_refs[turn - 1][...] = part.astype(BF16)
        else:
            own_ref[...] = part


def block_grad_kernel(acts_ref, own_ref, *refs):
    part_refs, (features_ref, grad_ref) = refs[:-2], refs[-2:]
    blocks, width = grad_ref.shape[0], grad_ref.shape[-1]
    total = own_ref[...]
    for part_ref in part_refs:
        total = total + part_ref[...].astype(F32)
    features = total.astype(BF16)
    features_ref[...] = features
    acts = acts_ref[...]
    for block in range(blocks):
        cols = slice(block * width, (block + 1) * width)
        grad_ref[block] = lax.dot_general(
            acts[:, cols], features[:, cols], (((0,), (0,)), ((), ())), preferred_element_type=F32
        )


def chain_kernel(gathered_ref, grad_ref, out_ref):
    shares, blocks, rows, width = gathered_ref.shape
    every = range(blocks)
    param = [gathered_ref[:, b].reshape(width, width) for b in every]
    skew = [param[b] - param[b].T for b in every]
    skew_pair = [split(skew[b]) for b in every]
    square = [product(skew_pair[b], skew_pair[b]) for b in every]
    square_pair = [split(square[b]) for b in every]
    grad = [grad_ref[b] for b in every]
    grad_pair = [split(grad[b]) for b in every]
    right_bar = [
        grad[b] + product(split(square[b] - 2.0 * skew[b]), grad_pair[b]) for b in every
    ]
    fourth = [product(square_pair[b], square_pair[b]) for b in every]
    left_bar = [grad[b] + product(grad_pair[b], split(square[b] + fourth[b])) for b in every]
    right_sym = [right_bar[b] + right_bar[b].T for b in every]
    both = [left_bar[b] + product(split(right_sym[b]), square_pair[b]) for b in every]
    square_sym = [right_sym[b] + both[b] + both[b].T for b in every]
    total = [2.0 * left_bar[b] - product(split(square_sym[b]), skew_pair[b]) for b in every]
    pieces = [(total[b] - total[b].T).reshape(shares, rows, width) for b in every]
    sends = jnp.concatenate(pieces, axis=1).astype(BF16)
    for place in range(shares):
        out_ref[place] = sends[shares - 1 - place]


def acts_kernel(gathered_ref, features_ref, out_ref):
    blocks, width = gathered_ref.shape[1], gathered_ref.shape[-1]
    for block in range(blocks):
        skew, _, square, _, rest = factors(gathered_ref, block)
        first = 2.0 * skew + square
        row = lax.broadcasted_iota(jnp.int32, (width, width), 0)
        col = lax.broadcasted_iota(jnp.int32, (width, width), 1)
        identity = jnp.where(row == col, 1.0, 0.0).astype(F32)
        rotation = (identity + first + rest + product(split(first), split(rest))).astype(BF16)
        cols = slice(block * width, (block + 1) * width)
        out_ref[:, cols] = lax.dot_general(
            features_ref[:, cols], rotation, (((1,), (1,)), ((), ())), preferred_element_type=F32
        ).astype(BF16)


def kernel_call(kernel, out_shape, flops, moved, **specs):
    return pl.pallas_call(
        kernel,
        out_shape=out_shape,
        compiler_params=pltpu.CompilerParams(vmem_limit_bytes=24 << 20),
        cost_estimate=pl.CostEstimate(flops=flops, bytes_accessed=moved, transcendentals=0),
        **specs,
    )


def body(activations, cotangent, base_weight, skew_param):
    shares = lax.axis_size("dp")
    parts = lax.axis_size("outcol")
    tokens, own_width = activations.shape
    depth = cotangent.shape[1]
    blocks, rows, width = skew_param.shape
    scale = 65536.0
    packed = (skew_param * scale).astype(jnp.float16).reshape(1, blocks * rows, width)
    descending = [list(range(shares - 1, -1, -1))]
    gathered = lax.all_to_all(
        jnp.broadcast_to(packed, (shares, blocks * rows, width)),
        "dp",
        0,
        0,
        axis_index_groups=descending,
        tiled=True,
    )
    gathered = (gathered.astype(F32) * (1.0 / scale)).reshape(shares, blocks, rows, width)[::-1]
    own, *sent = kernel_call(
        features_kernel,
        [jax.ShapeDtypeStruct((tokens, own_width), F32)]
        + [jax.ShapeDtypeStruct((tokens, own_width), BF16)] * (parts - 1),
        2 * tokens * depth * own_width * parts,
        2 << 20,
        in_specs=[pl.BlockSpec(memory_space=pltpu.VMEM), pl.BlockSpec(memory_space=pltpu.HBM)],
        scratch_shapes=[
            pltpu.VMEM((parts, own_width, depth), BF16),
            pltpu.SemaphoreType.DMA((parts,)),
        ],
    )(cotangent, pltpu.with_memory_space_constraint(base_weight, pltpu.HBM))
    received = [
        lax.ppermute(sent[turn - 1], "outcol", [(i, i ^ turn) for i in range(parts)])
        for turn in range(parts - 1, 0, -1)
    ]
    features, grad_rot = kernel_call(
        block_grad_kernel,
        (
            jax.ShapeDtypeStruct((tokens, own_width), BF16),
            jax.ShapeDtypeStruct((blocks, width, width), F32),
        ),
        2 * tokens * own_width * width,
        2 << 20,
    )(activations, own, *received)
    sends = kernel_call(
        chain_kernel,
        jax.ShapeDtypeStruct((shares, blocks * rows, width), BF16),
        2 * 18 * blocks * width**3,
        2 << 20,
    )(gathered, grad_rot)
    arrived = lax.all_to_all(sends, "dp", 0, 0, axis_index_groups=descending, tiled=True)
    grad_acts = kernel_call(
        acts_kernel,
        jax.ShapeDtypeStruct((tokens, own_width), BF16),
        2 * 10 * blocks * width**3,
        1 << 20,
    )(gathered, features)
    grad_skew = jnp.sum(arrived.astype(F32), axis=0).reshape(blocks, rows, width)
    return grad_acts, grad_skew


def solution(mesh):
    return jax.shard_map(
        body,
        mesh=mesh,
        in_specs=(
            P("dp", ("inblk", "outcol")),
            P("dp", "outcol"),
            P("inblk", "outcol"),
            P(("inblk", "outcol"), "dp", None),
        ),
        out_specs=(P("dp", ("inblk", "outcol")), P(("inblk", "outcol"), "dp", None)),
        check_vma=False,
    )
```

```python
import jax
import jax.numpy as jnp
from jax import lax
from jax.experimental import pallas as pl
from jax.experimental.pallas import tpu as pltpu
from jax.sharding import PartitionSpec as P

BF16 = jnp.bfloat16
F32 = jnp.float32


def split(x):
    high = x.astype(BF16)
    return high, (x - high.astype(F32)).astype(BF16)


def product(left, right):
    dot = lambda a, b: jnp.dot(a, b, preferred_element_type=F32)
    return dot(left[0], right[0]) + (dot(left[0], right[1]) + dot(left[1], right[0]))


def factors(gathered, block):
    shares = gathered.shape[0]
    param = jnp.concatenate(
        [gathered[shares - 1 - share, block] for share in range(shares)], axis=0
    )
    skew = param - param.T
    skew_pair = split(skew)
    square = product(skew_pair, skew_pair)
    square_pair = split(square)
    fourth = product(square_pair, square_pair)
    return skew, skew_pair, square, square_pair, square + fourth


def partial_sum(cotangent_ref, weight):
    return lax.dot_general(
        cotangent_ref[...], weight, (((1,), (1,)), ((), ())), preferred_element_type=F32
    )


def far_kernel(cotangent_ref, weight_ref, *refs):
    out_refs, held, semaphores = refs[:-2], refs[-2], refs[-1]
    width = held.shape[1]
    me = lax.axis_index("outcol")
    copies = []
    for place in range(len(out_refs)):
        first = pl.multiple_of((me ^ (3 - place)) * width, width)
        copies.append(
            pltpu.make_async_copy(
                weight_ref.at[pl.ds(first, width), :], held.at[place], semaphores.at[place]
            )
        )
        copies[place].start()
    for place, out_ref in enumerate(out_refs):
        copies[place].wait()
        out_ref[...] = partial_sum(cotangent_ref, held[place]).astype(BF16)


def near_kernel(cotangent_ref, weight_ref, sent_ref, own_ref):
    width = own_ref.shape[1]
    me = lax.axis_index("outcol")
    for turn, out_ref in ((1, sent_ref), (0, own_ref)):
        first = pl.multiple_of((me ^ turn) * width, width)
        part = partial_sum(cotangent_ref, weight_ref[pl.ds(first, width), :])
        out_ref[...] = part.astype(out_ref.dtype)


def powers_kernel(gathered_ref, *out_refs):
    shares, blocks, rows, width = gathered_ref.shape
    every = range(blocks)
    param = [
        jnp.concatenate([gathered_ref[shares - 1 - share, b] for share in range(shares)], axis=0)
        for b in every
    ]
    skew = [param[b] - param[b].T for b in every]
    skew_pair = [split(skew[b]) for b in every]
    square = [product(skew_pair[b], skew_pair[b]) for b in every]
    square_pair = [split(square[b]) for b in every]
    left_pair = [split(square[b] - 2.0 * skew[b]) for b in every]
    fourth = [product(square_pair[b], square_pair[b]) for b in every]
    rest_pair = [split(square[b] + fourth[b]) for b in every]
    for place, pair in enumerate((skew_pair, square_pair, left_pair, rest_pair)):
        for b in every:
            out_refs[2 * place][b] = pair[b][0]
            out_refs[2 * place + 1][b] = pair[b][1]


def chain_kernel(*refs):
    power_refs, (acts_ref, own_ref), part_refs = refs[:8], refs[8:10], refs[10:-2]
    features_ref, out_ref = refs[-2:]
    blocks, width, _ = power_refs[0].shape
    every = range(blocks)
    skew, square, left, rest = [
        [(power_refs[2 * place][b], power_refs[2 * place + 1][b]) for b in every]
        for place in range(4)
    ]
    features = own_ref[...]
    for part_ref in part_refs:
        features = features + part_ref[...].astype(F32)
    features = features.astype(BF16)
    features_ref[...] = features
    acts = acts_ref[...]
    cols = [slice(b * width, (b + 1) * width) for b in every]
    grad = [
        lax.dot_general(
            acts[:, cols[b]],
            features[:, cols[b]],
            (((0,), (0,)), ((), ())),
            preferred_element_type=F32,
        )
        for b in every
    ]
    grad_pair = [split(grad[b]) for b in every]
    right_bar = [grad[b] + product(left[b], grad_pair[b]) for b in every]
    left_bar = [grad[b] + product(grad_pair[b], rest[b]) for b in every]
    right_sym = [right_bar[b] + right_bar[b].T for b in every]
    both = [left_bar[b] + product(split(right_sym[b]), square[b]) for b in every]
    square_sym = [right_sym[b] + both[b] + both[b].T for b in every]
    total = [2.0 * left_bar[b] - product(split(square_sym[b]), skew[b]) for b in every]
    shares = out_ref.shape[0]
    pieces = [(total[b] - total[b].T).reshape(shares, -1, width) for b in every]
    sends = jnp.concatenate(pieces, axis=1).astype(BF16)
    for place in range(shares):
        out_ref[place] = sends[shares - 1 - place]


def acts_kernel(gathered_ref, features_ref, out_ref):
    blocks, width = gathered_ref.shape[1], gathered_ref.shape[-1]
    for block in range(blocks):
        skew, _, square, _, rest = factors(gathered_ref, block)
        first = 2.0 * skew + square
        row = lax.broadcasted_iota(jnp.int32, (width, width), 0)
        col = lax.broadcasted_iota(jnp.int32, (width, width), 1)
        identity = jnp.where(row == col, 1.0, 0.0).astype(F32)
        rotation = (identity + first + rest + product(split(first), split(rest))).astype(BF16)
        cols = slice(block * width, (block + 1) * width)
        out_ref[:, cols] = lax.dot_general(
            features_ref[:, cols], rotation, (((1,), (1,)), ((), ())), preferred_element_type=F32
        ).astype(BF16)


def kernel_call(kernel, out_shape, flops, moved, **specs):
    return pl.pallas_call(
        kernel,
        out_shape=out_shape,
        compiler_params=pltpu.CompilerParams(vmem_limit_bytes=24 << 20),
        cost_estimate=pl.CostEstimate(flops=flops, bytes_accessed=moved, transcendentals=0),
        **specs,
    )


def body(activations, cotangent, base_weight, skew_param):
    shares = lax.axis_size("dp")
    parts = lax.axis_size("outcol")
    tokens, own_width = activations.shape
    depth = cotangent.shape[1]
    blocks, rows, width = skew_param.shape
    scale = 65536.0
    packed = (skew_param * scale).astype(jnp.float16).reshape(1, blocks * rows, width)
    descending = [list(range(shares - 1, -1, -1))]
    gathered = lax.all_to_all(
        jnp.broadcast_to(packed, (shares, blocks * rows, width)),
        "dp",
        0,
        0,
        axis_index_groups=descending,
        tiled=True,
    )
    gathered = (gathered.astype(F32) * (1.0 / scale)).reshape(shares, blocks, rows, width)
    work = tokens * depth * own_width * parts
    far = kernel_call(
        far_kernel,
        [jax.ShapeDtypeStruct((tokens, own_width), BF16)] * 2,
        work,
        1 << 20,
        in_specs=[pl.BlockSpec(memory_space=pltpu.VMEM), pl.BlockSpec(memory_space=pltpu.HBM)],
        scratch_shapes=[
            pltpu.VMEM((2, own_width, depth), BF16),
            pltpu.SemaphoreType.DMA((2,)),
        ],
    )(cotangent, pltpu.with_memory_space_constraint(base_weight, pltpu.HBM))
    near, own = kernel_call(
        near_kernel,
        (
            jax.ShapeDtypeStruct((tokens, own_width), BF16),
            jax.ShapeDtypeStruct((tokens, own_width), F32),
        ),
        work,
        1 << 20,
    )(cotangent, base_weight)
    received = [
        lax.ppermute(part, "outcol", [(i, i ^ turn) for i in range(parts)])
        for turn, part in ((3, far[0]), (2, far[1]), (1, near))
    ]
    powers = kernel_call(
        powers_kernel,
        [jax.ShapeDtypeStruct((blocks, width, width), BF16)] * 8,
        2 * 6 * blocks * width**3,
        2 << 20,
    )(gathered)
    features, sends = kernel_call(
        chain_kernel,
        (
            jax.ShapeDtypeStruct((tokens, own_width), BF16),
            jax.ShapeDtypeStruct((shares, blocks * rows, width), BF16),
        ),
        2 * 12 * blocks * width**3,
        2 << 20,
    )(*powers, activations, own, *received)
    arrived = lax.all_to_all(sends, "dp", 0, 0, axis_index_groups=descending, tiled=True)
    grad_acts = kernel_call(
        acts_kernel,
        jax.ShapeDtypeStruct((tokens, own_width), BF16),
        2 * 10 * blocks * width**3,
        1 << 20,
    )(gathered, features)
    grad_skew = jnp.sum(arrived.astype(F32), axis=0).reshape(blocks, rows, width)
    return grad_acts, grad_skew


def solution(mesh):
    return jax.shard_map(
        body,
        mesh=mesh,
        in_specs=(
            P("dp", ("inblk", "outcol")),
            P("dp", "outcol"),
            P("inblk", "outcol"),
            P(("inblk", "outcol"), "dp", None),
        ),
        out_specs=(P("dp", ("inblk", "outcol")), P(("inblk", "outcol"), "dp", None)),
        check_vma=False,
    )
```

```python
import jax
import jax.numpy as jnp
from jax import lax
from jax.experimental import pallas as pl
from jax.experimental.pallas import tpu as pltpu
from jax.sharding import PartitionSpec as P

BF16 = jnp.bfloat16
F32 = jnp.float32


def split(x):
    high = x.astype(BF16)
    return high, (x - high.astype(F32)).astype(BF16)


def product(left, right):
    dot = lambda a, b: jnp.dot(a, b, preferred_element_type=F32)
    return dot(left[0], right[0]) + (dot(left[0], right[1]) + dot(left[1], right[0]))


def factors(gathered, block):
    shares = gathered.shape[0]
    param = jnp.concatenate(
        [gathered[shares - 1 - share, block] for share in range(shares)], axis=0
    )
    skew = param - param.T
    skew_pair = split(skew)
    square = product(skew_pair, skew_pair)
    square_pair = split(square)
    fourth = product(square_pair, square_pair)
    return skew, skew_pair, square, square_pair, square + fourth


def partial_sum(cotangent_ref, weight):
    return lax.dot_general(
        cotangent_ref[...], weight, (((1,), (1,)), ((), ())), preferred_element_type=F32
    )


def far_kernel(cotangent_ref, weight_ref, out_ref, cotangent, weight, semaphores):
    width = out_ref.shape[1]
    first = pl.multiple_of((lax.axis_index("outcol") ^ 3) * width, width)
    copies = [
        pltpu.make_async_copy(weight_ref.at[pl.ds(first, width), :], weight, semaphores.at[0]),
        pltpu.make_async_copy(cotangent_ref, cotangent, semaphores.at[1]),
    ]
    for copy in copies:
        copy.start()
    for copy in copies:
        copy.wait()
    out_ref[...] = partial_sum(cotangent, weight[...]).astype(BF16)


def near_kernel(cotangent_ref, weight_ref, *out_refs):
    width = out_refs[0].shape[1]
    me = lax.axis_index("outcol")
    for turn, out_ref in zip((2, 1, 0), out_refs):
        first = pl.multiple_of((me ^ turn) * width, width)
        part = partial_sum(cotangent_ref, weight_ref[pl.ds(first, width), :])
        out_ref[...] = part.astype(out_ref.dtype)


def powers_kernel(gathered_ref, *out_refs):
    shares, blocks, rows, width = gathered_ref.shape
    every = range(blocks)
    param = [
        jnp.concatenate([gathered_ref[shares - 1 - share, b] for share in range(shares)], axis=0)
        for b in every
    ]
    skew = [param[b] - param[b].T for b in every]
    skew_pair = [split(skew[b]) for b in every]
    square = [product(skew_pair[b], skew_pair[b]) for b in every]
    square_pair = [split(square[b]) for b in every]
    left_pair = [split(square[b] - 2.0 * skew[b]) for b in every]
    fourth = [product(square_pair[b], square_pair[b]) for b in every]
    rest_pair = [split(square[b] + fourth[b]) for b in every]
    for place, pair in enumerate((skew_pair, square_pair, left_pair, rest_pair)):
        for b in every:
            out_refs[2 * place][b] = pair[b][0]
            out_refs[2 * place + 1][b] = pair[b][1]


def chain_kernel(*refs):
    power_refs, (acts_ref, own_ref), part_refs = refs[:8], refs[8:10], refs[10:-2]
    features_ref, out_ref = refs[-2:]
    blocks, width, _ = power_refs[0].shape
    every = range(blocks)
    skew, square, left, rest = [
        [(power_refs[2 * place][b], power_refs[2 * place + 1][b]) for b in every]
        for place in range(4)
    ]
    features = own_ref[...]
    for part_ref in part_refs:
        features = features + part_ref[...].astype(F32)
    features = features.astype(BF16)
    features_ref[...] = features
    acts = acts_ref[...]
    cols = [slice(b * width, (b + 1) * width) for b in every]
    grad = [
        lax.dot_general(
            acts[:, cols[b]],
            features[:, cols[b]],
            (((0,), (0,)), ((), ())),
            preferred_element_type=F32,
        )
        for b in every
    ]
    grad_pair = [split(grad[b]) for b in every]
    right_bar = [grad[b] + product(left[b], grad_pair[b]) for b in every]
    left_bar = [grad[b] + product(grad_pair[b], rest[b]) for b in every]
    right_sym = [right_bar[b] + right_bar[b].T for b in every]
    both = [left_bar[b] + product(split(right_sym[b]), square[b]) for b in every]
    square_sym = [right_sym[b] + both[b] + both[b].T for b in every]
    total = [2.0 * left_bar[b] - product(split(square_sym[b]), skew[b]) for b in every]
    shares = out_ref.shape[0]
    pieces = [(total[b] - total[b].T).reshape(shares, -1, width) for b in every]
    sends = jnp.concatenate(pieces, axis=1).astype(BF16)
    for place in range(shares):
        out_ref[place] = sends[shares - 1 - place]


def acts_kernel(gathered_ref, features_ref, out_ref):
    blocks, width = gathered_ref.shape[1], gathered_ref.shape[-1]
    for block in range(blocks):
        skew, _, square, _, rest = factors(gathered_ref, block)
        first = 2.0 * skew + square
        row = lax.broadcasted_iota(jnp.int32, (width, width), 0)
        col = lax.broadcasted_iota(jnp.int32, (width, width), 1)
        identity = jnp.where(row == col, 1.0, 0.0).astype(F32)
        rotation = (identity + first + rest + product(split(first), split(rest))).astype(BF16)
        cols = slice(block * width, (block + 1) * width)
        out_ref[:, cols] = lax.dot_general(
            features_ref[:, cols], rotation, (((1,), (1,)), ((), ())), preferred_element_type=F32
        ).astype(BF16)


def kernel_call(kernel, out_shape, flops, moved, **specs):
    return pl.pallas_call(
        kernel,
        out_shape=out_shape,
        compiler_params=pltpu.CompilerParams(vmem_limit_bytes=24 << 20),
        cost_estimate=pl.CostEstimate(flops=flops, bytes_accessed=moved, transcendentals=0),
        **specs,
    )


def body(activations, cotangent, base_weight, skew_param):
    shares = lax.axis_size("dp")
    parts = lax.axis_size("outcol")
    tokens, own_width = activations.shape
    depth = cotangent.shape[1]
    blocks, rows, width = skew_param.shape
    scale = 65536.0
    packed = (skew_param * scale).astype(jnp.float16).reshape(1, blocks * rows, width)
    descending = [list(range(shares - 1, -1, -1))]
    gathered = lax.all_to_all(
        jnp.broadcast_to(packed, (shares, blocks * rows, width)),
        "dp",
        0,
        0,
        axis_index_groups=descending,
        tiled=True,
    )
    gathered = (gathered.astype(F32) * (1.0 / scale)).reshape(shares, blocks, rows, width)
    work = tokens * depth * own_width * parts
    in_hbm = pl.BlockSpec(memory_space=pltpu.HBM)
    chunk = jax.ShapeDtypeStruct((tokens, own_width), BF16)
    far = kernel_call(
        far_kernel,
        chunk,
        work // 2,
        1 << 19,
        in_specs=[in_hbm, in_hbm],
        scratch_shapes=[
            pltpu.VMEM((tokens, depth), BF16),
            pltpu.VMEM((own_width, depth), BF16),
            pltpu.SemaphoreType.DMA((2,)),
        ],
    )(
        pltpu.with_memory_space_constraint(cotangent, pltpu.HBM),
        pltpu.with_memory_space_constraint(base_weight, pltpu.HBM),
    )
    side, near, own = kernel_call(
        near_kernel,
        (chunk, chunk, jax.ShapeDtypeStruct((tokens, own_width), F32)),
        work + work // 2,
        1 << 20,
    )(cotangent, base_weight)
    received = [
        lax.ppermute(part, "outcol", [(i, i ^ turn) for i in range(parts)])
        for turn, part in ((3, far), (2, side), (1, near))
    ]
    powers = kernel_call(
        powers_kernel,
        [jax.ShapeDtypeStruct((blocks, width, width), BF16)] * 8,
        2 * 6 * blocks * width**3,
        2 << 20,
    )(gathered)
    features, sends = kernel_call(
        chain_kernel,
        (
            jax.ShapeDtypeStruct((tokens, own_width), BF16),
            jax.ShapeDtypeStruct((shares, blocks * rows, width), BF16),
        ),
        2 * 12 * blocks * width**3,
        2 << 20,
    )(*powers, activations, own, *received)
    arrived = lax.all_to_all(sends, "dp", 0, 0, axis_index_groups=descending, tiled=True)
    grad_acts = kernel_call(
        acts_kernel,
        jax.ShapeDtypeStruct((tokens, own_width), BF16),
        2 * 10 * blocks * width**3,
        1 << 20,
    )(gathered, features)
    grad_skew = jnp.sum(arrived.astype(F32), axis=0).reshape(blocks, rows, width)
    return grad_acts, grad_skew


def solution(mesh):
    return jax.shard_map(
        body,
        mesh=mesh,
        in_specs=(
            P("dp", ("inblk", "outcol")),
            P("dp", "outcol"),
            P("inblk", "outcol"),
            P(("inblk", "outcol"), "dp", None),
        ),
        out_specs=(P("dp", ("inblk", "outcol")), P(("inblk", "outcol"), "dp", None)),
        check_vma=False,
    )
```

```python
import jax
import jax.numpy as jnp
from jax import lax
from jax.experimental import pallas as pl
from jax.experimental.pallas import tpu as pltpu
from jax.sharding import PartitionSpec as P

BF16 = jnp.bfloat16
F32 = jnp.float32


def split(x):
    high = x.astype(BF16)
    return high, (x - high.astype(F32)).astype(BF16)


def product(left, right):
    dot = lambda a, b: jnp.dot(a, b, preferred_element_type=F32)
    return dot(left[0], right[0]) + (dot(left[0], right[1]) + dot(left[1], right[0]))


def last_order(shares):
    rows = [list(range(first, first + 8)) for first in range(0, shares, 8)]
    return [share for row in rows[::-1] for share in row[3::-1] + row[:3:-1]]


def factors(gathered, block):
    shares = gathered.shape[0]
    param = jnp.concatenate(
        [gathered[shares - 1 - share, block] for share in range(shares)], axis=0
    )
    skew = param - param.T
    skew_pair = split(skew)
    square = product(skew_pair, skew_pair)
    square_pair = split(square)
    fourth = product(square_pair, square_pair)
    return skew, skew_pair, square, square_pair, square + fourth


def partial_sum(cotangent_ref, weight):
    return lax.dot_general(
        cotangent_ref[...], weight, (((1,), (1,)), ((), ())), preferred_element_type=F32
    )


def far_kernel(cotangent_ref, weight_ref, out_ref, cotangent, weight, semaphores):
    width = out_ref.shape[1]
    first = pl.multiple_of((lax.axis_index("outcol") ^ 3) * width, width)
    copies = [
        pltpu.make_async_copy(weight_ref.at[pl.ds(first, width), :], weight, semaphores.at[0]),
        pltpu.make_async_copy(cotangent_ref, cotangent, semaphores.at[1]),
    ]
    for copy in copies:
        copy.start()
    for copy in copies:
        copy.wait()
    out_ref[...] = partial_sum(cotangent, weight[...]).astype(BF16)


def near_kernel(cotangent_ref, weight_ref, *out_refs):
    width = out_refs[0].shape[1]
    me = lax.axis_index("outcol")
    for turn, out_ref in zip((2, 1, 0), out_refs):
        first = pl.multiple_of((me ^ turn) * width, width)
        part = partial_sum(cotangent_ref, weight_ref[pl.ds(first, width), :])
        out_ref[...] = part.astype(out_ref.dtype)


def powers_kernel(gathered_ref, *out_refs):
    shares, blocks, rows, width = gathered_ref.shape
    every = range(blocks)
    param = [
        jnp.concatenate([gathered_ref[shares - 1 - share, b] for share in range(shares)], axis=0)
        for b in every
    ]
    skew = [param[b] - param[b].T for b in every]
    skew_pair = [split(skew[b]) for b in every]
    square = [product(skew_pair[b], skew_pair[b]) for b in every]
    square_pair = [split(square[b]) for b in every]
    left_pair = [split(square[b] - 2.0 * skew[b]) for b in every]
    fourth = [product(square_pair[b], square_pair[b]) for b in every]
    rest_pair = [split(square[b] + fourth[b]) for b in every]
    for place, pair in enumerate((skew_pair, square_pair, left_pair, rest_pair)):
        for b in every:
            out_refs[2 * place][b] = pair[b][0]
            out_refs[2 * place + 1][b] = pair[b][1]


def chain_kernel(*refs):
    power_refs, (acts_ref, own_ref), part_refs = refs[:8], refs[8:10], refs[10:-2]
    features_ref, out_ref = refs[-2:]
    blocks, width, _ = power_refs[0].shape
    every = range(blocks)
    skew, square, left, rest = [
        [(power_refs[2 * place][b], power_refs[2 * place + 1][b]) for b in every]
        for place in range(4)
    ]
    features = own_ref[...]
    for part_ref in part_refs:
        features = features + part_ref[...].astype(F32)
    features = features.astype(BF16)
    features_ref[...] = features
    acts = acts_ref[...]
    cols = [slice(b * width, (b + 1) * width) for b in every]
    grad = [
        lax.dot_general(
            acts[:, cols[b]],
            features[:, cols[b]],
            (((0,), (0,)), ((), ())),
            preferred_element_type=F32,
        )
        for b in every
    ]
    grad_pair = [split(grad[b]) for b in every]
    right_bar = [grad[b] + product(left[b], grad_pair[b]) for b in every]
    left_bar = [grad[b] + product(grad_pair[b], rest[b]) for b in every]
    right_sym = [right_bar[b] + right_bar[b].T for b in every]
    both = [left_bar[b] + product(split(right_sym[b]), square[b]) for b in every]
    square_sym = [right_sym[b] + both[b] + both[b].T for b in every]
    total = [2.0 * left_bar[b] - product(split(square_sym[b]), skew[b]) for b in every]
    shares = out_ref.shape[0]
    pieces = [(total[b] - total[b].T).reshape(shares, -1, width) for b in every]
    sends = jnp.concatenate(pieces, axis=1).astype(BF16)
    for place in range(shares):
        out_ref[place] = sends[last_order(shares)[place]]


def acts_kernel(gathered_ref, features_ref, out_ref):
    blocks, width = gathered_ref.shape[1], gathered_ref.shape[-1]
    for block in range(blocks):
        skew, _, square, _, rest = factors(gathered_ref, block)
        first = 2.0 * skew + square
        row = lax.broadcasted_iota(jnp.int32, (width, width), 0)
        col = lax.broadcasted_iota(jnp.int32, (width, width), 1)
        identity = jnp.where(row == col, 1.0, 0.0).astype(F32)
        rotation = (identity + first + rest + product(split(first), split(rest))).astype(BF16)
        cols = slice(block * width, (block + 1) * width)
        out_ref[:, cols] = lax.dot_general(
            features_ref[:, cols], rotation, (((1,), (1,)), ((), ())), preferred_element_type=F32
        ).astype(BF16)


def kernel_call(kernel, out_shape, flops, moved, **specs):
    return pl.pallas_call(
        kernel,
        out_shape=out_shape,
        compiler_params=pltpu.CompilerParams(vmem_limit_bytes=24 << 20),
        cost_estimate=pl.CostEstimate(flops=flops, bytes_accessed=moved, transcendentals=0),
        **specs,
    )


def body(activations, cotangent, base_weight, skew_param):
    shares = lax.axis_size("dp")
    parts = lax.axis_size("outcol")
    tokens, own_width = activations.shape
    depth = cotangent.shape[1]
    blocks, rows, width = skew_param.shape
    scale = 65536.0
    packed = (skew_param * scale).astype(jnp.float16).reshape(1, blocks * rows, width)
    descending = [list(range(shares - 1, -1, -1))]
    gathered = lax.all_to_all(
        jnp.broadcast_to(packed, (shares, blocks * rows, width)),
        "dp",
        0,
        0,
        axis_index_groups=descending,
        tiled=True,
    )
    gathered = (gathered.astype(F32) * (1.0 / scale)).reshape(shares, blocks, rows, width)
    work = tokens * depth * own_width * parts
    in_hbm = pl.BlockSpec(memory_space=pltpu.HBM)
    chunk = jax.ShapeDtypeStruct((tokens, own_width), BF16)
    far = kernel_call(
        far_kernel,
        chunk,
        work // 2,
        1 << 19,
        in_specs=[in_hbm, in_hbm],
        scratch_shapes=[
            pltpu.VMEM((tokens, depth), BF16),
            pltpu.VMEM((own_width, depth), BF16),
            pltpu.SemaphoreType.DMA((2,)),
        ],
    )(
        pltpu.with_memory_space_constraint(cotangent, pltpu.HBM),
        pltpu.with_memory_space_constraint(base_weight, pltpu.HBM),
    )
    side, near, own = kernel_call(
        near_kernel,
        (chunk, chunk, jax.ShapeDtypeStruct((tokens, own_width), F32)),
        work + work // 2,
        1 << 20,
    )(cotangent, base_weight)
    received = [
        lax.ppermute(part, "outcol", [(i, i ^ turn) for i in range(parts)])
        for turn, part in ((3, far), (2, side), (1, near))
    ]
    powers = kernel_call(
        powers_kernel,
        [jax.ShapeDtypeStruct((blocks, width, width), BF16)] * 8,
        2 * 6 * blocks * width**3,
        2 << 20,
    )(gathered)
    features, sends = kernel_call(
        chain_kernel,
        (
            jax.ShapeDtypeStruct((tokens, own_width), BF16),
            jax.ShapeDtypeStruct((shares, blocks * rows, width), BF16),
        ),
        2 * 12 * blocks * width**3,
        2 << 20,
    )(*powers, activations, own, *received)
    arrived = lax.all_to_all(sends, "dp", 0, 0, axis_index_groups=[last_order(shares)], tiled=True)
    grad_acts = kernel_call(
        acts_kernel,
        jax.ShapeDtypeStruct((tokens, own_width), BF16),
        2 * 10 * blocks * width**3,
        1 << 20,
    )(gathered, features)
    grad_skew = jnp.sum(arrived.astype(F32), axis=0).reshape(blocks, rows, width)
    return grad_acts, grad_skew


def solution(mesh):
    return jax.shard_map(
        body,
        mesh=mesh,
        in_specs=(
            P("dp", ("inblk", "outcol")),
            P("dp", "outcol"),
            P("inblk", "outcol"),
            P(("inblk", "outcol"), "dp", None),
        ),
        out_specs=(P("dp", ("inblk", "outcol")), P(("inblk", "outcol"), "dp", None)),
        check_vma=False,
    )
```

```python
import jax
import jax.numpy as jnp
from jax import lax
from jax.experimental import pallas as pl
from jax.experimental.pallas import tpu as pltpu
from jax.sharding import PartitionSpec as P

BF16 = jnp.bfloat16
F32 = jnp.float32


def split(x):
    high = x.astype(BF16)
    return high, (x - high.astype(F32)).astype(BF16)


def product(left, right):
    dot = lambda a, b: jnp.dot(a, b, preferred_element_type=F32)
    return dot(left[0], right[0]) + (dot(left[0], right[1]) + dot(left[1], right[0]))


def last_order(shares):
    rows = [list(range(first, first + 8)) for first in range(0, shares, 8)]
    rows = rows[0::2][::-1] + rows[1::2][::-1]
    return [share for row in rows for share in row[3::-1] + row[:3:-1]]


def factors(gathered, block):
    shares = gathered.shape[0]
    param = jnp.concatenate(
        [gathered[shares - 1 - share, block] for share in range(shares)], axis=0
    )
    skew = param - param.T
    skew_pair = split(skew)
    square = product(skew_pair, skew_pair)
    square_pair = split(square)
    fourth = product(square_pair, square_pair)
    return skew, skew_pair, square, square_pair, square + fourth


def partial_sum(cotangent_ref, weight):
    return lax.dot_general(
        cotangent_ref[...], weight, (((1,), (1,)), ((), ())), preferred_element_type=F32
    )


def far_kernel(cotangent_ref, weight_ref, out_ref, cotangent, weight, semaphores):
    width = out_ref.shape[1]
    first = pl.multiple_of((lax.axis_index("outcol") ^ 3) * width, width)
    copies = [
        pltpu.make_async_copy(weight_ref.at[pl.ds(first, width), :], weight, semaphores.at[0]),
        pltpu.make_async_copy(cotangent_ref, cotangent, semaphores.at[1]),
    ]
    for copy in copies:
        copy.start()
    for copy in copies:
        copy.wait()
    out_ref[...] = partial_sum(cotangent, weight[...]).astype(BF16)


def near_kernel(cotangent_ref, weight_ref, *out_refs):
    width = out_refs[0].shape[1]
    me = lax.axis_index("outcol")
    for turn, out_ref in zip((2, 1, 0), out_refs):
        first = pl.multiple_of((me ^ turn) * width, width)
        part = partial_sum(cotangent_ref, weight_ref[pl.ds(first, width), :])
        out_ref[...] = part.astype(out_ref.dtype)


def powers_kernel(gathered_ref, *out_refs):
    shares, blocks, rows, width = gathered_ref.shape
    every = range(blocks)
    param = [
        jnp.concatenate([gathered_ref[shares - 1 - share, b] for share in range(shares)], axis=0)
        for b in every
    ]
    skew = [param[b] - param[b].T for b in every]
    skew_pair = [split(skew[b]) for b in every]
    square = [product(skew_pair[b], skew_pair[b]) for b in every]
    square_pair = [split(square[b]) for b in every]
    left_pair = [split(square[b] - 2.0 * skew[b]) for b in every]
    fourth = [product(square_pair[b], square_pair[b]) for b in every]
    rest_pair = [split(square[b] + fourth[b]) for b in every]
    for place, pair in enumerate((skew_pair, square_pair, left_pair, rest_pair)):
        for b in every:
            out_refs[2 * place][b] = pair[b][0]
            out_refs[2 * place + 1][b] = pair[b][1]


def chain_kernel(*refs):
    power_refs, (acts_ref, own_ref), part_refs = refs[:8], refs[8:10], refs[10:-2]
    features_ref, out_ref = refs[-2:]
    blocks, width, _ = power_refs[0].shape
    every = range(blocks)
    skew, square, left, rest = [
        [(power_refs[2 * place][b], power_refs[2 * place + 1][b]) for b in every]
        for place in range(4)
    ]
    features = own_ref[...]
    for part_ref in part_refs:
        features = features + part_ref[...].astype(F32)
    features = features.astype(BF16)
    features_ref[...] = features
    acts = acts_ref[...]
    cols = [slice(b * width, (b + 1) * width) for b in every]
    grad = [
        lax.dot_general(
            acts[:, cols[b]],
            features[:, cols[b]],
            (((0,), (0,)), ((), ())),
            preferred_element_type=F32,
        )
        for b in every
    ]
    grad_pair = [split(grad[b]) for b in every]
    right_bar = [grad[b] + product(left[b], grad_pair[b]) for b in every]
    left_bar = [grad[b] + product(grad_pair[b], rest[b]) for b in every]
    right_sym = [right_bar[b] + right_bar[b].T for b in every]
    both = [left_bar[b] + product(split(right_sym[b]), square[b]) for b in every]
    square_sym = [right_sym[b] + both[b] + both[b].T for b in every]
    total = [2.0 * left_bar[b] - product(split(square_sym[b]), skew[b]) for b in every]
    shares = out_ref.shape[0]
    pieces = [(total[b] - total[b].T).reshape(shares, -1, width) for b in every]
    sends = jnp.concatenate(pieces, axis=1).astype(BF16)
    for place in range(shares):
        out_ref[place] = sends[last_order(shares)[place]]


def acts_kernel(gathered_ref, features_ref, out_ref):
    blocks, width = gathered_ref.shape[1], gathered_ref.shape[-1]
    for block in range(blocks):
        skew, _, square, _, rest = factors(gathered_ref, block)
        first = 2.0 * skew + square
        row = lax.broadcasted_iota(jnp.int32, (width, width), 0)
        col = lax.broadcasted_iota(jnp.int32, (width, width), 1)
        identity = jnp.where(row == col, 1.0, 0.0).astype(F32)
        rotation = (identity + first + rest + product(split(first), split(rest))).astype(BF16)
        cols = slice(block * width, (block + 1) * width)
        out_ref[:, cols] = lax.dot_general(
            features_ref[:, cols], rotation, (((1,), (1,)), ((), ())), preferred_element_type=F32
        ).astype(BF16)


def kernel_call(kernel, out_shape, flops, moved, **specs):
    return pl.pallas_call(
        kernel,
        out_shape=out_shape,
        compiler_params=pltpu.CompilerParams(vmem_limit_bytes=24 << 20),
        cost_estimate=pl.CostEstimate(flops=flops, bytes_accessed=moved, transcendentals=0),
        **specs,
    )


def body(activations, cotangent, base_weight, skew_param):
    shares = lax.axis_size("dp")
    parts = lax.axis_size("outcol")
    tokens, own_width = activations.shape
    depth = cotangent.shape[1]
    blocks, rows, width = skew_param.shape
    scale = 65536.0
    packed = (skew_param * scale).astype(jnp.float16).reshape(1, blocks * rows, width)
    descending = [list(range(shares - 1, -1, -1))]
    gathered = lax.all_to_all(
        jnp.broadcast_to(packed, (shares, blocks * rows, width)),
        "dp",
        0,
        0,
        axis_index_groups=descending,
        tiled=True,
    )
    gathered = (gathered.astype(F32) * (1.0 / scale)).reshape(shares, blocks, rows, width)
    work = tokens * depth * own_width * parts
    in_hbm = pl.BlockSpec(memory_space=pltpu.HBM)
    chunk = jax.ShapeDtypeStruct((tokens, own_width), BF16)
    far = kernel_call(
        far_kernel,
        chunk,
        work // 2,
        1 << 19,
        in_specs=[in_hbm, in_hbm],
        scratch_shapes=[
            pltpu.VMEM((tokens, depth), BF16),
            pltpu.VMEM((own_width, depth), BF16),
            pltpu.SemaphoreType.DMA((2,)),
        ],
    )(
        pltpu.with_memory_space_constraint(cotangent, pltpu.HBM),
        pltpu.with_memory_space_constraint(base_weight, pltpu.HBM),
    )
    side, near, own = kernel_call(
        near_kernel,
        (chunk, chunk, jax.ShapeDtypeStruct((tokens, own_width), F32)),
        work + work // 2,
        1 << 20,
    )(cotangent, base_weight)
    received = [
        lax.ppermute(part, "outcol", [(i, i ^ turn) for i in range(parts)])
        for turn, part in ((3, far), (2, side), (1, near))
    ]
    powers = kernel_call(
        powers_kernel,
        [jax.ShapeDtypeStruct((blocks, width, width), BF16)] * 8,
        2 * 6 * blocks * width**3,
        2 << 20,
    )(gathered)
    features, sends = kernel_call(
        chain_kernel,
        (
            jax.ShapeDtypeStruct((tokens, own_width), BF16),
            jax.ShapeDtypeStruct((shares, blocks * rows, width), BF16),
        ),
        2 * 12 * blocks * width**3,
        2 << 20,
    )(*powers, activations, own, *received)
    arrived = lax.all_to_all(sends, "dp", 0, 0, axis_index_groups=[last_order(shares)], tiled=True)
    grad_acts = kernel_call(
        acts_kernel,
        jax.ShapeDtypeStruct((tokens, own_width), BF16),
        2 * 10 * blocks * width**3,
        1 << 20,
    )(gathered, features)
    grad_skew = jnp.sum(arrived.astype(F32), axis=0).reshape(blocks, rows, width)
    return grad_acts, grad_skew


def solution(mesh):
    return jax.shard_map(
        body,
        mesh=mesh,
        in_specs=(
            P("dp", ("inblk", "outcol")),
            P("dp", "outcol"),
            P("inblk", "outcol"),
            P(("inblk", "outcol"), "dp", None),
        ),
        out_specs=(P("dp", ("inblk", "outcol")), P(("inblk", "outcol"), "dp", None)),
        check_vma=False,
    )
```

```python
import jax
import jax.numpy as jnp
from jax import lax
from jax.experimental import pallas as pl
from jax.experimental.pallas import tpu as pltpu
from jax.sharding import PartitionSpec as P

BF16 = jnp.bfloat16
F32 = jnp.float32


def split(x):
    high = x.astype(BF16)
    return high, (x - high.astype(F32)).astype(BF16)


def product(left, right):
    dot = lambda a, b: jnp.dot(a, b, preferred_element_type=F32)
    return dot(left[0], right[0]) + (dot(left[0], right[1]) + dot(left[1], right[0]))


def first_order(shares):
    return [8*y+z for y in (1, 0, 3, 2) for z in (7, 6, 5, 4, 3, 2, 1, 0)]


def last_order(shares):
    return [8*y+z for y in (2, 0, 3, 1) for z in (3, 7, 2, 6, 1, 5, 0, 4)]


def factors(gathered, block):
    shares = gathered.shape[0]
    param = jnp.concatenate(
        [gathered[first_order(shares).index(share), block] for share in range(shares)], axis=0
    )
    skew = param - param.T
    skew_pair = split(skew)
    square = product(skew_pair, skew_pair)
    square_pair = split(square)
    fourth = product(square_pair, square_pair)
    return skew, skew_pair, square, square_pair, square + fourth


def partial_sum(cotangent_ref, weight):
    return lax.dot_general(
        cotangent_ref[...], weight, (((1,), (1,)), ((), ())), preferred_element_type=F32
    )


def far_kernel(cotangent_ref, weight_ref, out_ref, cotangent, weight, semaphores):
    width = out_ref.shape[1]
    first = pl.multiple_of((lax.axis_index("outcol") ^ 3) * width, width)
    copies = [
        pltpu.make_async_copy(weight_ref.at[pl.ds(first, width), :], weight, semaphores.at[0]),
        pltpu.make_async_copy(cotangent_ref, cotangent, semaphores.at[1]),
    ]
    for copy in copies:
        copy.start()
    for copy in copies:
        copy.wait()
    out_ref[...] = partial_sum(cotangent, weight[...]).astype(BF16)


def near_kernel(cotangent_ref, weight_ref, *out_refs):
    width = out_refs[0].shape[1]
    me = lax.axis_index("outcol")
    for turn, out_ref in zip((2, 1, 0), out_refs):
        first = pl.multiple_of((me ^ turn) * width, width)
        part = partial_sum(cotangent_ref, weight_ref[pl.ds(first, width), :])
        out_ref[...] = part.astype(out_ref.dtype)


def powers_kernel(gathered_ref, *out_refs):
    shares, blocks, rows, width = gathered_ref.shape
    every = range(blocks)
    param = [
        jnp.concatenate([gathered_ref[first_order(shares).index(share), b] for share in range(shares)], axis=0)
        for b in every
    ]
    skew = [param[b] - param[b].T for b in every]
    skew_pair = [split(skew[b]) for b in every]
    square = [product(skew_pair[b], skew_pair[b]) for b in every]
    square_pair = [split(square[b]) for b in every]
    left_pair = [split(square[b] - 2.0 * skew[b]) for b in every]
    fourth = [product(square_pair[b], square_pair[b]) for b in every]
    rest_pair = [split(square[b] + fourth[b]) for b in every]
    for place, pair in enumerate((skew_pair, square_pair, left_pair, rest_pair)):
        for b in every:
            out_refs[2 * place][b] = pair[b][0]
            out_refs[2 * place + 1][b] = pair[b][1]


def chain_kernel(*refs):
    power_refs, (acts_ref, own_ref), part_refs = refs[:8], refs[8:10], refs[10:-2]
    features_ref, out_ref = refs[-2:]
    blocks, width, _ = power_refs[0].shape
    every = range(blocks)
    skew, square, left, rest = [
        [(power_refs[2 * place][b], power_refs[2 * place + 1][b]) for b in every]
        for place in range(4)
    ]
    features = own_ref[...]
    for part_ref in part_refs:
        features = features + part_ref[...].astype(F32)
    features = features.astype(BF16)
    features_ref[...] = features
    acts = acts_ref[...]
    cols = [slice(b * width, (b + 1) * width) for b in every]
    grad = [
        lax.dot_general(
            acts[:, cols[b]],
            features[:, cols[b]],
            (((0,), (0,)), ((), ())),
            preferred_element_type=F32,
        )
        for b in every
    ]
    grad_pair = [split(grad[b]) for b in every]
    right_bar = [grad[b] + product(left[b], grad_pair[b]) for b in every]
    left_bar = [grad[b] + product(grad_pair[b], rest[b]) for b in every]
    right_sym = [right_bar[b] + right_bar[b].T for b in every]
    both = [left_bar[b] + product(split(right_sym[b]), square[b]) for b in every]
    square_sym = [right_sym[b] + both[b] + both[b].T for b in every]
    total = [2.0 * left_bar[b] - product(split(square_sym[b]), skew[b]) for b in every]
    shares = out_ref.shape[0]
    pieces = [(total[b] - total[b].T).reshape(shares, -1, width) for b in every]
    sends = jnp.concatenate(pieces, axis=1).astype(BF16)
    for place in range(shares):
        out_ref[place] = sends[last_order(shares)[place]]


def acts_kernel(gathered_ref, features_ref, out_ref):
    blocks, width = gathered_ref.shape[1], gathered_ref.shape[-1]
    for block in range(blocks):
        skew, _, square, _, rest = factors(gathered_ref, block)
        first = 2.0 * skew + square
        row = lax.broadcasted_iota(jnp.int32, (width, width), 0)
        col = lax.broadcasted_iota(jnp.int32, (width, width), 1)
        identity = jnp.where(row == col, 1.0, 0.0).astype(F32)
        rotation = (identity + first + rest + product(split(first), split(rest))).astype(BF16)
        cols = slice(block * width, (block + 1) * width)
        out_ref[:, cols] = lax.dot_general(
            features_ref[:, cols], rotation, (((1,), (1,)), ((), ())), preferred_element_type=F32
        ).astype(BF16)


def kernel_call(kernel, out_shape, flops, moved, **specs):
    return pl.pallas_call(
        kernel,
        out_shape=out_shape,
        compiler_params=pltpu.CompilerParams(vmem_limit_bytes=24 << 20),
        cost_estimate=pl.CostEstimate(flops=flops, bytes_accessed=moved, transcendentals=0),
        **specs,
    )


def body(activations, cotangent, base_weight, skew_param):
    shares = lax.axis_size("dp")
    parts = lax.axis_size("outcol")
    tokens, own_width = activations.shape
    depth = cotangent.shape[1]
    blocks, rows, width = skew_param.shape
    scale = 65536.0
    packed = (skew_param * scale).astype(jnp.float16).reshape(1, blocks * rows, width)
    gathered = lax.all_to_all(
        jnp.broadcast_to(packed, (shares, blocks * rows, width)),
        "dp",
        0,
        0,
        axis_index_groups=[first_order(shares)],
        tiled=True,
    )
    gathered = (gathered.astype(F32) * (1.0 / scale)).reshape(shares, blocks, rows, width)
    work = tokens * depth * own_width * parts
    in_hbm = pl.BlockSpec(memory_space=pltpu.HBM)
    chunk = jax.ShapeDtypeStruct((tokens, own_width), BF16)
    far = kernel_call(
        far_kernel,
        chunk,
        work // 2,
        1 << 19,
        in_specs=[in_hbm, in_hbm],
        scratch_shapes=[
            pltpu.VMEM((tokens, depth), BF16),
            pltpu.VMEM((own_width, depth), BF16),
            pltpu.SemaphoreType.DMA((2,)),
        ],
    )(
        pltpu.with_memory_space_constraint(cotangent, pltpu.HBM),
        pltpu.with_memory_space_constraint(base_weight, pltpu.HBM),
    )
    side, near, own = kernel_call(
        near_kernel,
        (chunk, chunk, jax.ShapeDtypeStruct((tokens, own_width), F32)),
        work + work // 2,
        1 << 20,
    )(cotangent, base_weight)
    received = [
        lax.ppermute(part, "outcol", [(i, i ^ turn) for i in range(parts)])
        for turn, part in ((3, far), (2, side), (1, near))
    ]
    powers = kernel_call(
        powers_kernel,
        [jax.ShapeDtypeStruct((blocks, width, width), BF16)] * 8,
        2 * 6 * blocks * width**3,
        2 << 20,
    )(gathered)
    features, sends = kernel_call(
        chain_kernel,
        (
            jax.ShapeDtypeStruct((tokens, own_width), BF16),
            jax.ShapeDtypeStruct((shares, blocks * rows, width), BF16),
        ),
        2 * 12 * blocks * width**3,
        2 << 20,
    )(*powers, activations, own, *received)
    arrived = lax.all_to_all(sends, "dp", 0, 0, axis_index_groups=[last_order(shares)], tiled=True)
    grad_acts = kernel_call(
        acts_kernel,
        jax.ShapeDtypeStruct((tokens, own_width), BF16),
        2 * 10 * blocks * width**3,
        1 << 20,
    )(gathered, features)
    grad_skew = jnp.sum(arrived.astype(F32), axis=0).reshape(blocks, rows, width)
    return grad_acts, grad_skew


def solution(mesh):
    return jax.shard_map(
        body,
        mesh=mesh,
        in_specs=(
            P("dp", ("inblk", "outcol")),
            P("dp", "outcol"),
            P("inblk", "outcol"),
            P(("inblk", "outcol"), "dp", None),
        ),
        out_specs=(P("dp", ("inblk", "outcol")), P(("inblk", "outcol"), "dp", None)),
        check_vma=False,
    )
```
